512 devices in a mesh: dp: 64 (over z, x, core), expert: 8 (over y).
Axes of the slice: x: 4, y: 8, z: 8, core: 2. Of those that a mesh axis runs over, the one named last changes fastest.
Arguments:
- tokens: bfloat16 [512, 2048], P('dp'), may hold values from -6 to 6
- expert_ids: int32 [512, 2], P('dp'), may hold values from 0 to 15, all different within a row; in each aligned block of 8 rows (0 to 7, 8 to 15, ...) at most 2 rows name the same one
- gate_levels: int32 [512, 2], P('dp'), may hold values from 1 to 1023
- w_gate: bfloat16 [16, 2048, 8192], P('expert', None, 'dp'), may hold values from -0.125 to 0.125
- w_up: bfloat16 [16, 2048, 8192], P('expert', None, 'dp'), may hold values from -0.125 to 0.125
- w_down: bfloat16 [16, 8192, 2048], P('expert', 'dp'), may hold values from -0.0625 to 0.0625
Outputs:
- moe_out: bfloat16 [512, 2048], P('dp')
The draws below stay inside these ranges and needn't reach their ends.
Inputs may be any that keep to these rules, and one draw needn't show every extreme that they name: `expert_ids`: the two experts of a token differ. Among the 8 rows of one index of dp (rows i * 8 to (i + 1) * 8 - 1) no expert is named by more than 2 rows, a bound that some block reaches.
All inputs are finite; a program needn't handle non-finite values.
Results may differ from the reference program's by a relative error of at most 0.0049.
Values may be sent and summed in bfloat16 or wider, within the bound.
A program may use at most 64 MiB of HBM per device.

```python
import math
import jax
import jax.numpy as jnp
import numpy as np
from jax import lax

D = 2048
FF = 8192
TOP = 2
TOK_DEV = 8
EXPERTS = 16
SLOTS = 2
TOKENS = 512
N_DP = 64


def plant(drawn, own_key, low, largest):
    spot = [jax.random.randint(jax.random.fold_in(own_key, axis), (), 0, length) for axis, length in enumerate(drawn.shape)]
    longest = drawn.shape.index(max(drawn.shape))
    neighbour = spot[:longest] + [(spot[longest] + 1) % drawn.shape[longest]] + spot[longest + 1:]
    return drawn.at[tuple(spot)].set(low).at[tuple(neighbour)].set(largest)


def steps_of(key, extent, split, least, largest):
    gain, own = 1.0, jax.random.fold_in(key, 6)
    for position, blocks in split:
        draws = jnp.exp(jax.random.uniform(jax.random.fold_in(own, position), (blocks,), jnp.float32, least / len(split), largest / len(split)))
        gain = gain * jnp.repeat(draws, extent[position] // blocks).reshape([-1 if axis == position else 1 for axis in range(len(extent))])
    return gain


def deal_out(key, own, number, rows, amount, top, most, slope):
    sequence = jax.random.permutation(key, amount)
    heavy_load, usual = load_shares(amount, rows * top, most, slope, True), load_shares(amount, rows * top, most, slope, False)
    places = jnp.arange(amount)

    def named(tallies, turn):
        used = int((tallies > 0).sum())
        fixed = max(1, used // 4)
        shifted = fixed + (places - fixed + turn * (used - fixed)) % max(1, amount - fixed)
        return jnp.zeros((amount,), jnp.int32).at[sequence[jnp.where(places < fixed, places, shifted)]].set(jnp.asarray(tallies, jnp.int32))

    tallies = jnp.where(number % 4 == 0, named(heavy_load, number // 4), named(usual, number - number // 4 - 1))
    mixed = jax.random.permutation(jax.random.fold_in(own, 3), amount)
    source_of, taker = mixed[0:amount // 2 * 2:2], mixed[1:amount // 2 * 2:2]
    room = jnp.minimum(tallies[source_of] - 1, most - tallies[taker]) // 2
    room = jnp.where((source_of == sequence[0]) | (taker == sequence[0]) | (tallies[taker] == 0), 0, jnp.maximum(room, 0))
    shifted = jax.random.randint(jax.random.fold_in(own, 4), (amount // 2,), 0, 1 << 20) % (room + 1)
    tallies = tallies.at[source_of].add(-shifted).at[taker].add(shifted)
    items = jnp.searchsorted(jnp.cumsum(tallies), jnp.arange(rows * top), side="right").astype(jnp.int32)
    grid = items.reshape(top, rows).T
    grid = grid[jax.random.permutation(jax.random.fold_in(own, 1), rows)]
    turn = jax.random.randint(jax.random.fold_in(own, 2), (rows, 1), 0, top)
    return jnp.take_along_axis(grid, (jnp.arange(top)[None, :] + turn) % top, axis=1)


def load_shares(amount, total, limit, skew, full):
    portions = [(1 << 20) // math.isqrt(grade ** skew) + 1 for grade in range(1, amount + 1)]
    largest = limit if full else min(limit, max(-(-total // amount), total * portions[0] // sum(portions)))
    least = 1 if total - largest >= amount - 1 else 0
    counts, rest = [largest] + [least] * (amount - 1), total - largest - least * (amount - 1)
    while rest > 0:
        candidates = [i for i in range(1, amount) if counts[i] < largest] or [i for i in range(1, amount) if counts[i] < limit]
        mass, left = sum([portions[i] for i in candidates]), rest
        for i in candidates:
            extra = min(limit - counts[i], max(1, left * portions[i] // mass), rest)
            counts[i] = counts[i] + extra
            rest = rest - extra
    return np.array(counts)


def noise(own_key, dims, scale, bound, pieces=(), held_as=jnp.bfloat16):
    drawn = jax.random.normal(own_key, dims, jnp.float32) * scale
    if len(pieces) > 0:
        drawn = steps_of(own_key, dims, pieces, -0.22, 0.18) * drawn
    return jnp.clip(drawn, min=-bound, max=bound).astype(held_as)


def setup_inputs(seed: int = 0) -> dict:
    keys = jax.random.split(jax.random.key(seed), 7)
    tokens = noise(keys[0], (TOKENS, D), 1.0, 6.0, ((0, 64),))
    expert_ids_keys = jax.random.split(jax.random.fold_in(keys[1], 1), TOKENS // TOK_DEV)
    expert_ids_turns = jax.random.permutation(jax.random.fold_in(keys[1], 3), TOKENS // TOK_DEV)
    expert_ids = jax.vmap(lambda own, number: deal_out(jax.random.fold_in(keys[1], 2), own, number, TOK_DEV, EXPERTS, TOP, SLOTS, 2))(expert_ids_keys, expert_ids_turns).reshape((TOKENS, TOP))
    gate_levels = plant(jax.random.randint(keys[2], (TOKENS, TOP), 1, 1024), jax.random.fold_in(keys[2], 1), 1, 1023).astype(jnp.int32)
    w_gate = noise(keys[3], (EXPERTS, D, FF), D ** -0.5, 0.125, ((0, 8), (2, 64)))
    w_up = noise(keys[4], (EXPERTS, D, FF), D ** -0.5, 0.125, ((0, 8), (2, 64)))
    w_down = noise(keys[5], (EXPERTS, FF, D), FF ** -0.5, 0.0625, ((0, 8), (1, 64)))
    return dict(tokens=tokens, expert_ids=expert_ids, gate_levels=gate_levels, w_gate=w_gate, w_up=w_up, w_down=w_down)


def reference(tokens, expert_ids, gate_levels, w_gate, w_up, w_down):
    levels = gate_levels.astype(jnp.float32)
    gates = levels / jnp.sum(levels, axis=1, keepdims=True)
    pair_expert = expert_ids.reshape(-1).astype(jnp.int32)
    pair_gate = gates.reshape(-1)
    n_pairs = pair_expert.shape[0]
    capacity = SLOTS * N_DP

    def one_expert(combined, expert):
        found = jnp.nonzero(pair_expert == expert, size=capacity, fill_value=n_pairs)[0].astype(jnp.int32)
        occupied = found < n_pairs
        safe_pair = jnp.where(occupied, found, 0).astype(jnp.int32)
        token_index = (safe_pair // TOP).astype(jnp.int32)
        picked = jnp.where(occupied[:, None], tokens[token_index], jnp.zeros((), tokens.dtype)).astype(jnp.float32)
        gate_proj = jnp.dot(picked, w_gate[expert].astype(jnp.float32), precision=lax.Precision.HIGHEST)
        up_proj = jnp.dot(picked, w_up[expert].astype(jnp.float32), precision=lax.Precision.HIGHEST)
        hidden = (jax.nn.silu(gate_proj) * up_proj).astype(jnp.bfloat16)
        expert_out = jnp.dot(hidden.astype(jnp.float32), w_down[expert].astype(jnp.float32), precision=lax.Precision.HIGHEST)
        scaled = expert_out * (pair_gate[safe_pair] * occupied.astype(jnp.float32))[:, None]
        combined = combined + jax.ops.segment_sum(scaled, token_index, num_segments=TOKENS)
        return combined, None

    combined, _ = lax.scan(one_expert, jnp.zeros((TOKENS, D), jnp.float32), jnp.arange(EXPERTS, dtype=jnp.int32))
    return combined.astype(jnp.bfloat16)
```

```python
import functools

import jax
import jax.numpy as jnp
from jax import lax
from jax.experimental import pallas as pl
from jax.experimental.pallas import tpu as pltpu
from jax.sharding import PartitionSpec as P

NX = 4
MESH = pl.DeviceIdType.MESH
F32 = jnp.float32
BF16 = jnp.bfloat16


def moe_kernel(
    nz, ny, ids, levels, tok, w_gate, w_up, w_down, out,
    wgu, wd, comp, comp_in, mix, mix_in, grid, part, part_in, near, far_in, merged,
    x_in, z_out, z_in, fin, half_out, half_in,
    w_sem, c_s, c_r, zg_s, zg_r, xg_s, xg_r, xf_s, xf_r, pg_s, pg_r, ps_s, ps_r,
    xs_s, xs_r, zs_s, zs_r, y_s, y_r,
):
    dp = lax.axis_index("dp")
    y = lax.axis_index("expert")
    c = lax.rem(dp, 2)
    x = lax.rem(dp // 2, NX)
    z = dp // (2 * NX)
    oc = 1 - c
    half = tok.shape[1] // 2
    hz = nz // 2
    xl, xr, xo = lax.rem(x + NX - 1, NX), lax.rem(x + 1, NX), lax.rem(x + 2, NX)

    def dev(zz, xx, cc):
        return ((zz * NX + xx) * 2 + cc, y)

    partner, left, right = dev(z, x, oc), dev(z, xl, c), dev(z, xr, c)
    z_to = [dev(lax.rem(z + d, nz), x, c) for d in range(nz)]
    y_to = [(dp, lax.rem(y + d, ny)) for d in range(ny)]
    sent = []

    def desc(src, dst, s, r, to):
        return pltpu.make_async_remote_copy(
            src_ref=src, dst_ref=dst, send_sem=s, recv_sem=r, device_id=to, device_id_type=MESH
        )

    def send(src, dst, s, r, to):
        copy = desc(src, dst, s, r, to)
        copy.start()
        sent.append(copy)

    def arrived(dst, s, r, to):
        desc(dst, dst, s, r, to).wait_recv()

    n_own, ff = w_gate.shape[0], w_gate.shape[2]
    loads = []
    for l in range(n_own):
        loads += [
            pltpu.make_async_copy(w_gate.at[l], wgu.at[l, :, pl.ds(0, ff)], w_sem.at[3 * l]),
            pltpu.make_async_copy(w_up.at[l], wgu.at[l, :, pl.ds(ff, ff)], w_sem.at[3 * l + 1]),
            pltpu.make_async_copy(w_down.at[l], wd.at[pl.ds(l * ff, ff)], w_sem.at[3 * l + 2]),
        ]
    for load in loads:
        load.start()

    barrier = pltpu.get_barrier_semaphore()
    peers = [partner, left, right] + z_to[1:] + y_to[1:]
    for peer in peers:
        pl.semaphore_signal(barrier, inc=1, device_id=peer, device_id_type=MESH)

    n_rows = tok.shape[0]
    row = lax.broadcasted_iota(jnp.int32, (8, 128), 0)
    lane = lax.broadcasted_iota(jnp.int32, (8, 128), 1)
    expert_row = 2 * y + row // 4
    here_row = (row % 4) // 2 == c
    slot_row = row % 2
    expert_lane = 2 * (lane // 8) + (lane % 8) // 4
    here_lane = (lane % 4) // 2 == c
    slot_lane = lane % 2
    seen_row = jnp.zeros((8, 128), jnp.int32)
    seen_lane = jnp.zeros((8, 128), jnp.int32)
    weights = jnp.zeros((8, 128), F32)
    tokens = tok[...].astype(F32)
    compact = jnp.zeros((8, 2 * half), F32)
    for t in range(n_rows):
        id0 = jnp.full((8, 128), ids[t, 0], jnp.int32)
        id1 = jnp.full((8, 128), ids[t, 1], jnp.int32)
        lev0 = jnp.full((8, 128), levels[t, 0], jnp.int32).astype(F32)
        lev1 = jnp.full((8, 128), levels[t, 1], jnp.int32).astype(F32)
        hit = (id0 == expert_row) | (id1 == expert_row)
        take = hit & (seen_row == slot_row) & here_row
        seen_row = seen_row + hit.astype(jnp.int32)
        factor = jnp.where(take, 1.0, 0.0).astype(F32)[:, :1]
        compact = compact + factor * tokens[t : t + 1, :]
        hit0, hit1 = id0 == expert_lane, id1 == expert_lane
        hit = hit0 | hit1
        take = hit & (seen_lane == slot_lane) & here_lane & (row == t)
        seen_lane = seen_lane + hit.astype(jnp.int32)
        weights = jnp.where(take, jnp.where(hit0, lev0, lev1) / (lev0 + lev1), weights)
    comp[0] = compact[:, :half].astype(BF16)
    comp[1] = compact[:, half:].astype(BF16)
    mix[...] = weights

    pl.semaphore_wait(barrier, len(peers))

    send(comp.at[oc], comp_in, c_s.at[0], c_r.at[0], partner)
    send(mix, mix_in, c_s.at[1], c_r.at[1], partner)
    arrived(comp_in, c_s.at[0], c_r.at[0], partner)
    grid[c, x, z] = (comp[c].astype(F32) + comp_in[...].astype(F32)).astype(BF16)

    order = sorted(range(nz), key=lambda d: (min(d, nz - d), d))
    z_src = [lax.rem(z + nz - d, nz) for d in range(nz)]
    for d in order[1:]:
        send(grid.at[c, x, z], grid.at[c, x, z], zg_s.at[d], zg_r.at[d], z_to[d])

    def relay(i):
        d = order[i]
        side = i % 2
        src = grid.at[c, (xl, xr)[side], z_src[d]]
        to = (right, left)[side]
        arrived(src, xg_s.at[side, d], xg_r.at[side, d], to)
        send(src, src, xf_s.at[d], xf_r.at[d], to)

    lag = 3
    for i, d in enumerate(order):
        block = grid.at[c, x, z_src[d]]
        if i:
            arrived(block, zg_s.at[d], zg_r.at[d], z_to[d])
        send(block, block, xg_s.at[0, d], xg_r.at[0, d], right)
        send(block, block, xg_s.at[1, d], xg_r.at[1, d], left)
        if i >= lag:
            relay(i - lag)
    send(grid.at[c, x], grid.at[c, x], pg_s.at[0], pg_r.at[0], partner)
    for i in range(max(nz - lag, 0), nz):
        relay(i)

    def swap_in(k, xx):
        send(grid.at[c, xx], grid.at[c, xx], pg_s.at[k], pg_r.at[k], partner)

    for side, xx in ((0, xl), (1, xr)):
        for i, d in enumerate(order):
            if i % 2 != side:
                arrived(
                    grid.at[c, xx, z_src[d]], xg_s.at[side, d], xg_r.at[side, d], (right, left)[side]
                )
        swap_in(1 + side, xx)

    rows = nz * 8
    own_row = (lax.broadcasted_iota(jnp.int32, (rows, ff), 0) % 8) // 4

    def compute(k, xx):
        arrived(grid.at[oc, xx], pg_s.at[k], pg_r.at[k], partner)
        block0 = grid[0, xx].astype(F32).reshape(rows, half).astype(BF16)
        block1 = grid[1, xx].astype(F32).reshape(rows, half).astype(BF16)
        parts = []
        for l in range(n_own):
            both = jnp.dot(block0, wgu[l, :half, :], preferred_element_type=F32)
            both = both + jnp.dot(block1, wgu[l, half:, :], preferred_element_type=F32)
            gate, up = both[:, :ff], both[:, ff:]
            hidden = gate / (1.0 + jnp.exp(-gate)) * up
            parts.append(jnp.where(own_row == l, hidden, 0.0).astype(BF16))
        hidden = jnp.concatenate(parts, axis=1)
        for h in range(2):
            result = jnp.dot(
                hidden, wd[:, h * half : (h + 1) * half], preferred_element_type=F32
            )
            part[k, h] = result.reshape(nz, 8, half).astype(BF16)
        send(part.at[k, oc], part_in.at[k], ps_s.at[k], ps_r.at[k], partner)

    def pair_sum(k):
        arrived(part_in.at[k], ps_s.at[k], ps_r.at[k], partner)
        return part[k, c].astype(F32) + part_in[k].astype(F32)

    for load in loads:
        load.wait()
    compute(0, x)
    for d in order:
        far = grid.at[c, xo, z_src[d]]
        arrived(far, xf_s.at[d], xf_r.at[d], right)
    swap_in(3, xo)
    compute(1, xl)
    compute(2, xr)
    low, high = pl.ds(0, hz), pl.ds(hz, hz)
    near[0] = pair_sum(1).astype(BF16)
    send(near.at[0, low], x_in.at[1, low], xs_s.at[0], xs_r.at[0], left)
    near[1] = pair_sum(2).astype(BF16)
    send(near.at[1, high], x_in.at[0, high], xs_s.at[1], xs_r.at[1], right)
    compute(3, xo)
    near[2] = pair_sum(3).astype(BF16)
    send(near.at[2, low], far_in.at[0], xs_s.at[2], xs_r.at[2], right)
    send(near.at[2, high], far_in.at[1], xs_s.at[3], xs_r.at[3], left)
    total = pair_sum(0)
    arrived(far_in.at[0], xs_s.at[2], xs_r.at[2], right)
    merged[0] = (near[1, :hz].astype(F32) + far_in[0].astype(F32)).astype(BF16)
    send(merged.at[0], x_in.at[0, low], xs_s.at[4], xs_r.at[4], right)
    arrived(far_in.at[1], xs_s.at[3], xs_r.at[3], left)
    merged[1] = (near[0, hz:].astype(F32) + far_in[1].astype(F32)).astype(BF16)
    send(merged.at[1], x_in.at[1, high], xs_s.at[5], xs_r.at[5], left)
    arrived(x_in.at[1, low], xs_s.at[0], xs_r.at[0], left)
    arrived(x_in.at[0, high], xs_s.at[1], xs_r.at[1], right)
    arrived(x_in.at[0, low], xs_s.at[4], xs_r.at[4], right)
    arrived(x_in.at[1, high], xs_s.at[5], xs_r.at[5], left)
    z_out[...] = (total + x_in[0].astype(F32) + x_in[1].astype(F32)).astype(BF16)

    for d in reversed(order[1:]):
        send(z_out.at[lax.rem(z + d, nz)], z_in.at[d], zs_s.at[d], zs_r.at[d], z_to[d])
    final = z_out[z].astype(F32)
    for d in order[1:]:
        arrived(z_in.at[d], zs_s.at[d], zs_r.at[d], z_to[d])
        final = final + z_in[d].astype(F32)

    fin[y] = final.astype(BF16)
    y_order = sorted(range(1, ny), key=lambda d: -min(d, ny - d))
    for d in y_order:
        send(fin.at[y], fin.at[y], y_s.at[d], y_r.at[d], y_to[d])
    arrived(mix_in, c_s.at[1], c_r.at[1], partner)
    for d in reversed(y_order):
        arrived(fin.at[lax.rem(y + ny - d, ny)], y_s.at[d], y_r.at[d], y_to[d])
    values = fin[...].astype(F32).reshape(ny * 8, half)
    other = jnp.dot(
        mix_in[:, : ny * 8], values, precision=lax.Precision.HIGHEST, preferred_element_type=F32
    )
    half_out[...] = other.astype(BF16)
    send(half_out, half_in, c_s.at[2], c_r.at[2], partner)
    mine = jnp.dot(
        mix[:, : ny * 8], values, precision=lax.Precision.HIGHEST, preferred_element_type=F32
    )
    arrived(half_in, c_s.at[2], c_r.at[2], partner)
    theirs = half_in[...].astype(F32)
    out[:, :half] = jnp.where(c == 0, mine, theirs).astype(BF16)
    out[:, half:] = jnp.where(c == 0, theirs, mine).astype(BF16)
    for copy in sent:
        copy.wait_send()


def on_device(nz, ny, tokens, expert_ids, gate_levels, w_gate, w_up, w_down):
    width = tokens.shape[1]
    half = width // 2
    n_own, _, ff = w_gate.shape
    hz = nz // 2
    vmem, smem, dma = pltpu.VMEM, pltpu.SMEM, pltpu.SemaphoreType.DMA
    scratch = [
        vmem((n_own, width, 2 * ff), BF16),
        vmem((n_own * ff, width), BF16),
        vmem((2, 8, half), BF16),
        vmem((8, half), BF16),
        vmem((8, 128), F32),
        vmem((8, 128), F32),
        vmem((2, NX, nz, 8, half), BF16),
        vmem((4, 2, nz, 8, half), BF16),
        vmem((4, nz, 8, half), BF16),
        vmem((3, nz, 8, half), BF16),
        vmem((2, hz, 8, half), BF16),
        vmem((2, hz, 8, half), BF16),
        vmem((2, nz, 8, half), BF16),
        vmem((nz, 8, half), BF16),
        vmem((nz, 8, half), BF16),
        vmem((ny, 8, half), BF16),
        vmem((8, half), BF16),
        vmem((8, half), BF16),
        dma((3 * n_own,)),
        dma((3,)), dma((3,)),
        dma((nz,)), dma((nz,)),
        dma((2, nz)), dma((2, nz)),
        dma((nz,)), dma((nz,)),
        dma((4,)), dma((4,)),
        dma((4,)), dma((4,)),
        dma((6,)), dma((6,)),
        dma((nz,)), dma((nz,)),
        dma((ny,)), dma((ny,)),
    ]
    return pl.pallas_call(
        functools.partial(moe_kernel, nz, ny),
        out_shape=jax.ShapeDtypeStruct(tokens.shape, BF16),
        in_specs=[
            pl.BlockSpec(memory_space=smem),
            pl.BlockSpec(memory_space=smem),
            pl.BlockSpec(memory_space=vmem),
            pl.BlockSpec(memory_space=pl.ANY),
            pl.BlockSpec(memory_space=pl.ANY),
            pl.BlockSpec(memory_space=pl.ANY),
        ],
        out_specs=pl.BlockSpec(memory_space=vmem),
        scratch_shapes=scratch,
        compiler_params=pltpu.CompilerParams(
            collective_id=0, has_side_effects=True, vmem_limit_bytes=40 * 1024 * 1024
        ),
    )(expert_ids, gate_levels, tokens, w_gate, w_up, w_down)


def solution(mesh):
    nz = mesh.shape["dp"] // (2 * NX)
    in_specs = (
        P("dp", None),
        P("dp", None),
        P("dp", None),
        P("expert", None, "dp"),
        P("expert", None, "dp"),
        P("expert", "dp", None),
    )
    return jax.shard_map(
        functools.partial(on_device, nz, mesh.shape["expert"]),
        mesh=mesh, in_specs=in_specs, out_specs=P("dp", None), check_vma=False,
    )
```

```python
import functools

import jax
import jax.numpy as jnp
from jax import lax
from jax.experimental import pallas as pl
from jax.experimental.pallas import tpu as pltpu
from jax.sharding import PartitionSpec as P

NX = 4
Q = 2
MESH = pl.DeviceIdType.MESH
F32 = jnp.float32
BF16 = jnp.bfloat16


def moe_kernel(
    nz, ny, ids_hbm, levels_hbm, tok_hbm, w_gate, w_up, w_down, out,
    ids, levels, tok, wgu, wd, comp, comp_in, mix, mix_in, grid, part, part_in, near, far_in, merged,
    x_in, z_out, z_in, fin, half_out, half_in,
    in_sem, w_sem, c_s, c_r, zg_s, zg_r, xg_s, xg_r, xf_s, xf_r, pg_s, pg_r, ps_s, ps_r,
    xs_s, xs_r, zs_s, zs_r, y_s, y_r,
):
    dp = lax.axis_index("dp")
    y = lax.axis_index("expert")
    c = lax.rem(dp, 2)
    x = lax.rem(dp // 2, NX)
    z = dp // (2 * NX)
    oc = 1 - c
    half = tok.shape[1] // 2
    quarter = half // Q
    hz = nz // 2
    xl, xr, xo = lax.rem(x + NX - 1, NX), lax.rem(x + 1, NX), lax.rem(x + 2, NX)

    def dev(zz, xx, cc):
        return ((zz * NX + xx) * 2 + cc, y)

    partner, left, right = dev(z, x, oc), dev(z, xl, c), dev(z, xr, c)
    z_to = [dev(lax.rem(z + d, nz), x, c) for d in range(nz)]
    y_to = [(dp, lax.rem(y + d, ny)) for d in range(ny)]
    sent = []

    def desc(src, dst, s, r, to):
        return pltpu.make_async_remote_copy(
            src_ref=src, dst_ref=dst, send_sem=s, recv_sem=r, device_id=to, device_id_type=MESH
        )

    def send(src, dst, s, r, to):
        copy = desc(src, dst, s, r, to)
        copy.start()
        sent.append(copy)

    def arrived(dst, s, r, to):
        desc(dst, dst, s, r, to).wait_recv()

    small = [
        pltpu.make_async_copy(ids_hbm, ids, in_sem.at[0]),
        pltpu.make_async_copy(levels_hbm, levels, in_sem.at[1]),
        pltpu.make_async_copy(tok_hbm, tok, in_sem.at[2]),
    ]
    for load in small:
        load.start()

    barrier = pltpu.get_barrier_semaphore()
    peers = [partner, left, right] + z_to[1:] + y_to[1:]
    for peer in peers:
        pl.semaphore_signal(barrier, inc=1, device_id=peer, device_id_type=MESH)

    n_own, ff = w_gate.shape[0], w_gate.shape[2]
    loads = []
    for l in range(n_own):
        loads += [
            pltpu.make_async_copy(w_gate.at[l], wgu.at[l, :, pl.ds(0, ff)], w_sem.at[4 * l]),
            pltpu.make_async_copy(w_up.at[l], wgu.at[l, :, pl.ds(ff, ff)], w_sem.at[4 * l + 1]),
        ]
        for h in range(2):
            loads.append(
                pltpu.make_async_copy(
                    w_down.at[l, :, pl.ds(h * half, half)],
                    wd.at[h, pl.ds(l * ff, ff)],
                    w_sem.at[4 * l + 2 + h],
                )
            )
    for load in loads:
        load.start()
    for load in small:
        load.wait()

    n_rows = tok.shape[0]
    row = lax.broadcasted_iota(jnp.int32, (8, 128), 0)
    lane = lax.broadcasted_iota(jnp.int32, (8, 128), 1)
    expert_row = 2 * y + row // 4
    here_row = (row % 4) // 2 == c
    slot_row = row % 2
    expert_lane = 2 * (lane // 8) + (lane % 8) // 4
    here_lane = (lane % 4) // 2 == c
    slot_lane = lane % 2
    seen = jnp.zeros((8, 128), jnp.int32)
    tokens = tok[...].astype(F32)
    compact = jnp.zeros((8, 2 * half), F32)
    for t in range(n_rows):
        id0 = jnp.full((8, 128), ids[0, t], jnp.int32)
        id1 = jnp.full((8, 128), ids[1, t], jnp.int32)
        hit = (id0 == expert_row) | (id1 == expert_row)
        take = hit & (seen == slot_row) & here_row
        seen = seen + hit.astype(jnp.int32)
        factor = jnp.where(take, 1.0, 0.0).astype(F32)[:, :1]
        compact = compact + factor * tokens[t : t + 1, :]
    comp[0] = compact[:, :half].astype(BF16)
    comp[1] = compact[:, half:].astype(BF16)

    pl.semaphore_wait(barrier, len(peers))

    send(comp.at[oc], comp_in, c_s.at[0], c_r.at[0], partner)
    arrived(comp_in, c_s.at[0], c_r.at[0], partner)
    grid[c, x, z] = (comp[c].astype(F32) + comp_in[...].astype(F32)).astype(BF16)

    order = sorted(range(nz), key=lambda d: (min(d, nz - d), d))
    z_src = [lax.rem(z + nz - d, nz) for d in range(nz)]
    for d in order[1:]:
        send(grid.at[c, x, z], grid.at[c, x, z], zg_s.at[d], zg_r.at[d], z_to[d])

    seen = jnp.zeros((8, 128), jnp.int32)
    weights = jnp.zeros((8, 128), F32)
    for t in range(n_rows):
        hit0 = jnp.full((8, 128), ids[0, t], jnp.int32) == expert_lane
        hit1 = jnp.full((8, 128), ids[1, t], jnp.int32) == expert_lane
        lev0 = jnp.full((8, 128), levels[0, t], jnp.int32).astype(F32)
        lev1 = jnp.full((8, 128), levels[1, t], jnp.int32).astype(F32)
        hit = hit0 | hit1
        take = hit & (seen == slot_lane) & here_lane & (row == t)
        seen = seen + hit.astype(jnp.int32)
        weights = jnp.where(take, jnp.where(hit0, lev0, lev1) / (lev0 + lev1), weights)
    mix[...] = weights
    send(mix, mix_in, c_s.at[1], c_r.at[1], partner)

    def relay(i):
        d = order[i]
        side = i % 2
        src = grid.at[c, (xl, xr)[side], z_src[d]]
        to = (right, left)[side]
        arrived(src, xg_s.at[side, d], xg_r.at[side, d], to)
        send(src, src, xf_s.at[d], xf_r.at[d], to)

    lag = 3
    for i, d in enumerate(order):
        block = grid.at[c, x, z_src[d]]
        if i:
            arrived(block, zg_s.at[d], zg_r.at[d], z_to[d])
        send(block, block, xg_s.at[0, d], xg_r.at[0, d], right)
        send(block, block, xg_s.at[1, d], xg_r.at[1, d], left)
        if i >= lag:
            relay(i - lag)
    send(grid.at[c, x], grid.at[c, x], pg_s.at[0], pg_r.at[0], partner)
    for i in range(max(nz - lag, 0), nz):
        relay(i)

    def swap_in(k, xx):
        send(grid.at[c, xx], grid.at[c, xx], pg_s.at[k], pg_r.at[k], partner)

    for side, xx in ((0, xl), (1, xr)):
        for i, d in enumerate(order):
            if i % 2 != side:
                arrived(
                    grid.at[c, xx, z_src[d]], xg_s.at[side, d], xg_r.at[side, d], (right, left)[side]
                )
        swap_in(1 + side, xx)

    rows = nz * 8
    own_row = (lax.broadcasted_iota(jnp.int32, (rows, ff), 0) % 8) // 4

    def compute(k, xx):
        arrived(grid.at[oc, xx], pg_s.at[k], pg_r.at[k], partner)
        block0 = grid[0, xx].astype(F32).reshape(rows, half).astype(BF16)
        block1 = grid[1, xx].astype(F32).reshape(rows, half).astype(BF16)
        parts = []
        for l in range(n_own):
            both = jnp.dot(block0, wgu[l, :half, :], preferred_element_type=F32)
            both = both + jnp.dot(block1, wgu[l, half:, :], preferred_element_type=F32)
            gate, up = both[:, :ff], both[:, ff:]
            hidden = gate / (1.0 + jnp.exp(-gate)) * up
            parts.append(jnp.where(own_row == l, hidden, 0.0).astype(BF16))
        hidden = jnp.concatenate(parts, axis=1)
        for h in (oc, c):
            result = jnp.dot(hidden, wd[h], preferred_element_type=F32).reshape(nz, 8, half)
            for q in range(Q):
                part[k, h, q] = result[:, :, q * quarter : (q + 1) * quarter].astype(BF16)
                if h is oc:
                    send(part.at[k, oc, q], part_in.at[k, q], ps_s.at[k, q], ps_r.at[k, q], partner)

    def pair_sum(k, q):
        arrived(part_in.at[k, q], ps_s.at[k, q], ps_r.at[k, q], partner)
        return part[k, c, q].astype(F32) + part_in[k, q].astype(F32)

    for load in loads:
        load.wait()
    compute(0, x)
    for d in order:
        far = grid.at[c, xo, z_src[d]]
        arrived(far, xf_s.at[d], xf_r.at[d], right)
    swap_in(3, xo)
    compute(1, xl)
    compute(2, xr)

    low, high = pl.ds(0, hz), pl.ds(hz, hz)
    for q in range(Q):
        near[0, q] = pair_sum(1, q).astype(BF16)
        send(near.at[0, q, low], x_in.at[1, q, low], xs_s.at[0, q], xs_r.at[0, q], left)
        near[1, q] = pair_sum(2, q).astype(BF16)
        send(near.at[1, q, high], x_in.at[0, q, high], xs_s.at[1, q], xs_r.at[1, q], right)
    compute(3, xo)
    for q in range(Q):
        near[2, q] = pair_sum(3, q).astype(BF16)
        send(near.at[2, q, low], far_in.at[0, q], xs_s.at[2, q], xs_r.at[2, q], right)
        send(near.at[2, q, high], far_in.at[1, q], xs_s.at[3, q], xs_r.at[3, q], left)
    for q in range(Q):
        arrived(far_in.at[0, q], xs_s.at[2, q], xs_r.at[2, q], right)
        merged[0, q] = (near[1, q, :hz].astype(F32) + far_in[0, q].astype(F32)).astype(BF16)
        send(merged.at[0, q], x_in.at[0, q, low], xs_s.at[4, q], xs_r.at[4, q], right)
        arrived(far_in.at[1, q], xs_s.at[3, q], xs_r.at[3, q], left)
        merged[1, q] = (near[0, q, hz:].astype(F32) + far_in[1, q].astype(F32)).astype(BF16)
        send(merged.at[1, q], x_in.at[1, q, high], xs_s.at[5, q], xs_r.at[5, q], left)

    for q in range(Q):
        total = pair_sum(0, q)
        arrived(x_in.at[1, q, low], xs_s.at[0, q], xs_r.at[0, q], left)
        arrived(x_in.at[0, q, high], xs_s.at[1, q], xs_r.at[1, q], right)
        arrived(x_in.at[0, q, low], xs_s.at[4, q], xs_r.at[4, q], right)
        arrived(x_in.at[1, q, high], xs_s.at[5, q], xs_r.at[5, q], left)
        z_out[q] = (total + x_in[0, q].astype(F32) + x_in[1, q].astype(F32)).astype(BF16)
        for d in reversed(order[1:]):
            send(
                z_out.at[q, lax.rem(z + d, nz)], z_in.at[q, d], zs_s.at[q, d], zs_r.at[q, d], z_to[d]
            )

    y_order = sorted(range(1, ny), key=lambda d: -min(d, ny - d))
    for q in range(Q):
        final = z_out[q, z].astype(F32)
        for d in order[1:]:
            arrived(z_in.at[q, d], zs_s.at[q, d], zs_r.at[q, d], z_to[d])
            final = final + z_in[q, d].astype(F32)
        fin[q, y] = final.astype(BF16)
        for d in y_order:
            send(fin.at[q, y], fin.at[q, y], y_s.at[q, d], y_r.at[q, d], y_to[d])

    arrived(mix_in, c_s.at[1], c_r.at[1], partner)
    gates = jnp.concatenate([mix[...], mix_in[...]], axis=0)
    terms = []
    for _ in range(3):
        term = gates.astype(BF16).astype(F32)
        gates = gates - term
        terms.append(term)
    terms = jnp.concatenate(terms, axis=0)[:, : ny * 8].astype(BF16)
    mine = []
    for q in range(Q):
        for d in reversed(y_order):
            arrived(fin.at[q, lax.rem(y + ny - d, ny)], y_s.at[q, d], y_r.at[q, d], y_to[d])
        values = fin[q].astype(F32).reshape(ny * 8, quarter).astype(BF16)
        mixed = jnp.dot(terms, values, preferred_element_type=F32)
        mixed = mixed[32:] + mixed[16:32] + mixed[:16]
        half_out[q] = mixed[8:].astype(BF16)
        send(half_out.at[q], half_in.at[q], c_s.at[2 + q], c_r.at[2 + q], partner)
        mine.append(mixed[:8])
    for q in range(Q):
        arrived(half_in.at[q], c_s.at[2 + q], c_r.at[2 + q], partner)
        theirs = half_in[q].astype(F32)
        first, second = q * quarter, half + q * quarter
        out[:, first : first + quarter] = jnp.where(c == 0, mine[q], theirs).astype(BF16)
        out[:, second : second + quarter] = jnp.where(c == 0, theirs, mine[q]).astype(BF16)
    for copy in sent:
        copy.wait_send()


def on_device(nz, ny, tokens, expert_ids, gate_levels, w_gate, w_up, w_down):
    width = tokens.shape[1]
    half = width // 2
    n_own, _, ff = w_gate.shape
    hz = nz // 2
    vmem, smem, dma = pltpu.VMEM, pltpu.SMEM, pltpu.SemaphoreType.DMA
    quarter = half // Q
    scratch = [
        smem((2, tokens.shape[0]), jnp.int32),
        smem((2, tokens.shape[0]), jnp.int32),
        vmem(tokens.shape, BF16),
        vmem((n_own, width, 2 * ff), BF16),
        vmem((2, n_own * ff, half), BF16),
        vmem((2, 8, half), BF16),
        vmem((8, half), BF16),
        vmem((8, 128), F32),
        vmem((8, 128), F32),
        vmem((2, NX, nz, 8, half), BF16),
        vmem((4, 2, Q, nz, 8, quarter), BF16),
        vmem((4, Q, nz, 8, quarter), BF16),
        vmem((3, Q, nz, 8, quarter), BF16),
        vmem((2, Q, hz, 8, quarter), BF16),
        vmem((2, Q, hz, 8, quarter), BF16),
        vmem((2, Q, nz, 8, quarter), BF16),
        vmem((Q, nz, 8, quarter), BF16),
        vmem((Q, nz, 8, quarter), BF16),
        vmem((Q, ny, 8, quarter), BF16),
        vmem((Q, 8, quarter), BF16),
        vmem((Q, 8, quarter), BF16),
        dma((3,)),
        dma((4 * n_own,)),
        dma((2 + Q,)), dma((2 + Q,)),
        dma((nz,)), dma((nz,)),
        dma((2, nz)), dma((2, nz)),
        dma((nz,)), dma((nz,)),
        dma((4,)), dma((4,)),
        dma((4, Q)), dma((4, Q)),
        dma((6, Q)), dma((6, Q)),
        dma((Q, nz)), dma((Q, nz)),
        dma((Q, ny)), dma((Q, ny)),
    ]
    return pl.pallas_call(
        functools.partial(moe_kernel, nz, ny),
        out_shape=jax.ShapeDtypeStruct(tokens.shape, BF16),
        in_specs=[pl.BlockSpec(memory_space=pl.ANY)] * 6,
        out_specs=pl.BlockSpec(memory_space=vmem),
        scratch_shapes=scratch,
        compiler_params=pltpu.CompilerParams(
            collective_id=0, has_side_effects=True, vmem_limit_bytes=67043328
        ),
    )(expert_ids.T, gate_levels.T, tokens, w_gate, w_up, w_down)


def solution(mesh):
    nz = mesh.shape["dp"] // (2 * NX)
    in_specs = (
        P("dp", None),
        P("dp", None),
        P("dp", None),
        P("expert", None, "dp"),
        P("expert", None, "dp"),
        P("expert", "dp", None),
    )
    return jax.shard_map(
        functools.partial(on_device, nz, mesh.shape["expert"]),
        mesh=mesh, in_specs=in_specs, out_specs=P("dp", None), check_vma=False,
    )
```

```python
import functools

import jax
import jax.numpy as jnp
from jax import lax
from jax.experimental import pallas as pl
from jax.experimental.pallas import tpu as pltpu
from jax.sharding import PartitionSpec as P

NX = 4
Q = 2
MESH = pl.DeviceIdType.MESH
F32 = jnp.float32
BF16 = jnp.bfloat16


def moe_kernel(
    nz, ny, ids_hbm, levels_hbm, tok_hbm, w_gate, w_up, w_down, out,
    ids, levels, tok, wgu, wd, comp, comp_in, mix, mix_in, grid, part, part_in, near, far_in, merged,
    x_in, z_out, z_in, fin, half_out, half_in,
    in_sem, w_sem, c_s, c_r, zg_s, zg_r, xg_s, xg_r, xf_s, xf_r, pg_s, pg_r, ps_s, ps_r,
    xs_s, xs_r, zs_s, zs_r, y_s, y_r,
):
    dp = lax.axis_index("dp")
    y = lax.axis_index("expert")
    c = lax.rem(dp, 2)
    x = lax.rem(dp // 2, NX)
    z = dp // (2 * NX)
    oc = 1 - c
    half = tok.shape[1] // 2
    quarter = half // Q
    hz = nz // 2
    xl, xr, xo = lax.rem(x + NX - 1, NX), lax.rem(x + 1, NX), lax.rem(x + 2, NX)

    def dev(zz, xx, cc):
        return ((zz * NX + xx) * 2 + cc, y)

    partner, left, right = dev(z, x, oc), dev(z, xl, c), dev(z, xr, c)
    opposite = dev(z, xo, c)
    z_to = [dev(lax.rem(z + d, nz), x, c) for d in range(nz)]
    y_to = [(dp, lax.rem(y + d, ny)) for d in range(ny)]
    sent = []

    def desc(src, dst, s, r, to):
        return pltpu.make_async_remote_copy(
            src_ref=src, dst_ref=dst, send_sem=s, recv_sem=r, device_id=to, device_id_type=MESH
        )

    def send(src, dst, s, r, to):
        copy = desc(src, dst, s, r, to)
        copy.start()
        sent.append(copy)

    def arrived(dst, s, r, to):
        desc(dst, dst, s, r, to).wait_recv()

    small = [
        pltpu.make_async_copy(ids_hbm, ids, in_sem.at[0]),
        pltpu.make_async_copy(levels_hbm, levels, in_sem.at[1]),
        pltpu.make_async_copy(tok_hbm, tok, in_sem.at[2]),
    ]
    for load in small:
        load.start()

    barrier = pltpu.get_barrier_semaphore()
    peers = [partner, left, right, opposite] + z_to[1:] + y_to[1:]
    for peer in peers:
        pl.semaphore_signal(barrier, inc=1, device_id=peer, device_id_type=MESH)

    n_own, ff = w_gate.shape[0], w_gate.shape[2]
    loads = []
    for l in range(n_own):
        loads += [
            pltpu.make_async_copy(w_gate.at[l], wgu.at[l, :, pl.ds(0, ff)], w_sem.at[4 * l]),
            pltpu.make_async_copy(w_up.at[l], wgu.at[l, :, pl.ds(ff, ff)], w_sem.at[4 * l + 1]),
        ]
        for h in range(2):
            loads.append(
                pltpu.make_async_copy(
                    w_down.at[l, :, pl.ds(h * half, half)],
                    wd.at[h, pl.ds(l * ff, ff)],
                    w_sem.at[4 * l + 2 + h],
                )
            )
    for load in loads:
        load.start()
    for load in small:
        load.wait()

    n_rows = tok.shape[0]
    row = lax.broadcasted_iota(jnp.int32, (8, 128), 0)
    lane = lax.broadcasted_iota(jnp.int32, (8, 128), 1)
    expert_row = 2 * y + row // 4
    here_row = (row % 4) // 2 == c
    slot_row = row % 2
    expert_lane = 2 * (lane // 8) + (lane % 8) // 4
    here_lane = (lane % 4) // 2 == c
    slot_lane = lane % 2
    seen = jnp.zeros((8, 128), jnp.int32)
    tokens = tok[...].astype(F32)
    compact = jnp.zeros((8, 2 * half), F32)
    for t in range(n_rows):
        id0 = jnp.full((8, 128), ids[0, t], jnp.int32)
        id1 = jnp.full((8, 128), ids[1, t], jnp.int32)
        hit = (id0 == expert_row) | (id1 == expert_row)
        take = hit & (seen == slot_row) & here_row
        seen = seen + hit.astype(jnp.int32)
        factor = jnp.where(take, 1.0, 0.0).astype(F32)[:, :1]
        compact = compact + factor * tokens[t : t + 1, :]
    comp[0] = compact[:, :half].astype(BF16)
    comp[1] = compact[:, half:].astype(BF16)

    pl.semaphore_wait(barrier, len(peers))

    send(comp.at[oc], comp_in, c_s.at[0], c_r.at[0], partner)
    arrived(comp_in, c_s.at[0], c_r.at[0], partner)
    grid[c, x, z] = (comp[c].astype(F32) + comp_in[...].astype(F32)).astype(BF16)

    order = sorted(range(nz), key=lambda d: (min(d, nz - d), d))
    z_src = [lax.rem(z + nz - d, nz) for d in range(nz)]
    for d in reversed(order[1:]):
        send(grid.at[c, x, z], grid.at[c, x, z], zg_s.at[d], zg_r.at[d], z_to[d])

    seen = jnp.zeros((8, 128), jnp.int32)
    weights = jnp.zeros((8, 128), F32)
    for t in range(n_rows):
        hit0 = jnp.full((8, 128), ids[0, t], jnp.int32) == expert_lane
        hit1 = jnp.full((8, 128), ids[1, t], jnp.int32) == expert_lane
        lev0 = jnp.full((8, 128), levels[0, t], jnp.int32).astype(F32)
        lev1 = jnp.full((8, 128), levels[1, t], jnp.int32).astype(F32)
        hit = hit0 | hit1
        take = hit & (seen == slot_lane) & here_lane & (row == t)
        seen = seen + hit.astype(jnp.int32)
        weights = jnp.where(take, jnp.where(hit0, lev0, lev1) / (lev0 + lev1), weights)
    mix[...] = weights
    send(mix, mix_in, c_s.at[1], c_r.at[1], partner)

    def relay(i):
        d = order[i]
        side = i % 2
        src = grid.at[c, (xl, xr)[side], z_src[d]]
        to = (right, left)[side]
        arrived(src, xg_s.at[side, d], xg_r.at[side, d], to)
        send(src, src, xf_s.at[d], xf_r.at[d], to)

    lag = 3
    n_relay = min(nz, 5)
    for i, d in enumerate(order):
        block = grid.at[c, x, z_src[d]]
        if i:
            arrived(block, zg_s.at[d], zg_r.at[d], z_to[d])
        send(block, block, xg_s.at[0, d], xg_r.at[0, d], right)
        send(block, block, xg_s.at[1, d], xg_r.at[1, d], left)
        if i >= n_relay:
            send(block, block, xf_s.at[d], xf_r.at[d], opposite)
        if lag <= i < n_relay + lag:
            relay(i - lag)
    send(grid.at[c, x], grid.at[c, x], pg_s.at[0], pg_r.at[0], partner)
    for i in range(max(nz - lag, 0), n_relay):
        relay(i)

    def swap_in(k, xx):
        send(grid.at[c, xx], grid.at[c, xx], pg_s.at[k], pg_r.at[k], partner)

    for side, xx in ((0, xl), (1, xr)):
        for i, d in enumerate(order):
            if i % 2 != side or i >= n_relay:
                arrived(
                    grid.at[c, xx, z_src[d]], xg_s.at[side, d], xg_r.at[side, d], (right, left)[side]
                )
        swap_in(1 + side, xx)

    rows = nz * 8
    own_row = (lax.broadcasted_iota(jnp.int32, (rows, ff), 0) % 8) // 4

    def compute(k, xx):
        if k == 3:
            for d in order:
                far = grid.at[oc, xo, z_src[d]]
                arrived(far, pg_s.at[3 + d], pg_r.at[3 + d], partner)
        else:
            arrived(grid.at[oc, xx], pg_s.at[k], pg_r.at[k], partner)
        block0 = grid[0, xx].astype(F32).reshape(rows, half).astype(BF16)
        block1 = grid[1, xx].astype(F32).reshape(rows, half).astype(BF16)
        parts = []
        for l in range(n_own):
            both = jnp.dot(block0, wgu[l, :half, :], preferred_element_type=F32)
            both = both + jnp.dot(block1, wgu[l, half:, :], preferred_element_type=F32)
            gate, up = both[:, :ff], both[:, ff:]
            hidden = gate / (1.0 + jnp.exp(-gate)) * up
            parts.append(jnp.where(own_row == l, hidden, 0.0).astype(BF16))
        hidden = jnp.concatenate(parts, axis=1)
        for h in (oc, c):
            result = jnp.dot(hidden, wd[h], preferred_element_type=F32).reshape(nz, 8, half)
            for q in range(Q):
                part[k, h, q] = result[:, :, q * quarter : (q + 1) * quarter].astype(BF16)
                if h is oc:
                    send(part.at[k, oc, q], part_in.at[k, q], ps_s.at[k, q], ps_r.at[k, q], partner)

    def pair_sum(k, q):
        arrived(part_in.at[k, q], ps_s.at[k, q], ps_r.at[k, q], partner)
        return part[k, c, q].astype(F32) + part_in[k, q].astype(F32)

    for load in loads:
        load.wait()
    compute(0, x)
    for d in order:
        far = grid.at[c, xo, z_src[d]]
        arrived(far, xf_s.at[d], xf_r.at[d], right)
        send(far, far, pg_s.at[3 + d], pg_r.at[3 + d], partner)
    compute(1, xl)
    compute(2, xr)
    compute(3, xo)

    low, high = pl.ds(0, hz), pl.ds(hz, hz)
    def near_send(q):
        send(near.at[0, q, low], x_in.at[1, q, low], xs_s.at[0, q], xs_r.at[0, q], left)
        send(near.at[1, q, high], x_in.at[0, q, high], xs_s.at[1, q], xs_r.at[1, q], right)

    for q in range(Q):
        near[0, q] = pair_sum(1, q).astype(BF16)
        near[1, q] = pair_sum(2, q).astype(BF16)
        if q == 0:
            near_send(q)
    for q in range(Q):
        near[2, q] = pair_sum(3, q).astype(BF16)
        send(near.at[2, q, low], far_in.at[0, q], xs_s.at[2, q], xs_r.at[2, q], right)
        send(near.at[2, q, high], far_in.at[1, q], xs_s.at[3, q], xs_r.at[3, q], left)
    for q in range(1, Q):
        near_send(q)
    for q in range(Q):
        arrived(far_in.at[0, q], xs_s.at[2, q], xs_r.at[2, q], right)
        merged[0, q] = (near[1, q, :hz].astype(F32) + far_in[0, q].astype(F32)).astype(BF16)
        send(merged.at[0, q], x_in.at[0, q, low], xs_s.at[4, q], xs_r.at[4, q], right)
        arrived(far_in.at[1, q], xs_s.at[3, q], xs_r.at[3, q], left)
        merged[1, q] = (near[0, q, hz:].astype(F32) + far_in[1, q].astype(F32)).astype(BF16)
        send(merged.at[1, q], x_in.at[1, q, high], xs_s.at[5, q], xs_r.at[5, q], left)

    for q in range(Q):
        total = pair_sum(0, q)
        arrived(x_in.at[1, q, low], xs_s.at[0, q], xs_r.at[0, q], left)
        arrived(x_in.at[0, q, high], xs_s.at[1, q], xs_r.at[1, q], right)
        arrived(x_in.at[0, q, low], xs_s.at[4, q], xs_r.at[4, q], right)
        arrived(x_in.at[1, q, high], xs_s.at[5, q], xs_r.at[5, q], left)
        z_out[q] = (total + x_in[0, q].astype(F32) + x_in[1, q].astype(F32)).astype(BF16)
        for d in reversed(order[1:]):
            send(
                z_out.at[q, lax.rem(z + d, nz)], z_in.at[q, d], zs_s.at[q, d], zs_r.at[q, d], z_to[d]
            )

    y_order = sorted(range(1, ny), key=lambda d: -min(d, ny - d))
    for q in range(Q):
        final = z_out[q, z].astype(F32)
        for d in order[1:]:
            arrived(z_in.at[q, d], zs_s.at[q, d], zs_r.at[q, d], z_to[d])
            final = final + z_in[q, d].astype(F32)
        fin[q, y] = final.astype(BF16)
        for d in y_order:
            send(fin.at[q, y], fin.at[q, y], y_s.at[q, d], y_r.at[q, d], y_to[d])

    arrived(mix_in, c_s.at[1], c_r.at[1], partner)
    gates = jnp.concatenate([mix[...], mix_in[...]], axis=0)
    terms = []
    for _ in range(3):
        term = gates.astype(BF16).astype(F32)
        gates = gates - term
        terms.append(term)
    terms = jnp.concatenate(terms, axis=0)[:, : ny * 8].astype(BF16)
    mine = []
    for q in range(Q):
        for d in reversed(y_order):
            arrived(fin.at[q, lax.rem(y + ny - d, ny)], y_s.at[q, d], y_r.at[q, d], y_to[d])
        values = fin[q].astype(F32).reshape(ny * 8, quarter).astype(BF16)
        mixed = jnp.dot(terms, values, preferred_element_type=F32)
        mixed = mixed[32:] + mixed[16:32] + mixed[:16]
        half_out[q] = mixed[8:].astype(BF16)
        send(half_out.at[q], half_in.at[q], c_s.at[2 + q], c_r.at[2 + q], partner)
        mine.append(mixed[:8])
    for q in range(Q):
        arrived(half_in.at[q], c_s.at[2 + q], c_r.at[2 + q], partner)
        theirs = half_in[q].astype(F32)
        first, second = q * quarter, half + q * quarter
        out[:, first : first + quarter] = jnp.where(c == 0, mine[q], theirs).astype(BF16)
        out[:, second : second + quarter] = jnp.where(c == 0, theirs, mine[q]).astype(BF16)
    for copy in sent:
        copy.wait_send()


def on_device(nz, ny, tokens, expert_ids, gate_levels, w_gate, w_up, w_down):
    width = tokens.shape[1]
    half = width // 2
    n_own, _, ff = w_gate.shape
    hz = nz // 2
    vmem, smem, dma = pltpu.VMEM, pltpu.SMEM, pltpu.SemaphoreType.DMA
    quarter = half // Q
    scratch = [
        smem((2, tokens.shape[0]), jnp.int32),
        smem((2, tokens.shape[0]), jnp.int32),
        vmem(tokens.shape, BF16),
        vmem((n_own, width, 2 * ff), BF16),
        vmem((2, n_own * ff, half), BF16),
        vmem((2, 8, half), BF16),
        vmem((8, half), BF16),
        vmem((8, 128), F32),
        vmem((8, 128), F32),
        vmem((2, NX, nz, 8, half), BF16),
        vmem((4, 2, Q, nz, 8, quarter), BF16),
        vmem((4, Q, nz, 8, quarter), BF16),
        vmem((3, Q, nz, 8, quarter), BF16),
        vmem((2, Q, hz, 8, quarter), BF16),
        vmem((2, Q, hz, 8, quarter), BF16),
        vmem((2, Q, nz, 8, quarter), BF16),
        vmem((Q, nz, 8, quarter), BF16),
        vmem((Q, nz, 8, quarter), BF16),
        vmem((Q, ny, 8, quarter), BF16),
        vmem((Q, 8, quarter), BF16),
        vmem((Q, 8, quarter), BF16),
        dma((3,)),
        dma((4 * n_own,)),
        dma((2 + Q,)), dma((2 + Q,)),
        dma((nz,)), dma((nz,)),
        dma((2, nz)), dma((2, nz)),
        dma((nz,)), dma((nz,)),
        dma((3 + nz,)), dma((3 + nz,)),
        dma((4, Q)), dma((4, Q)),
        dma((6, Q)), dma((6, Q)),
        dma((Q, nz)), dma((Q, nz)),
        dma((Q, ny)), dma((Q, ny)),
    ]
    return pl.pallas_call(
        functools.partial(moe_kernel, nz, ny),
        out_shape=jax.ShapeDtypeStruct(tokens.shape, BF16),
        in_specs=[pl.BlockSpec(memory_space=pl.ANY)] * 6,
        out_specs=pl.BlockSpec(memory_space=vmem),
        scratch_shapes=scratch,
        compiler_params=pltpu.CompilerParams(
            collective_id=0, has_side_effects=True, vmem_limit_bytes=67043328
        ),
    )(expert_ids.T, gate_levels.T, tokens, w_gate, w_up, w_down)


def solution(mesh):
    nz = mesh.shape["dp"] // (2 * NX)
    in_specs = (
        P("dp", None),
        P("dp", None),
        P("dp", None),
        P("expert", None, "dp"),
        P("expert", None, "dp"),
        P("expert", "dp", None),
    )
    return jax.shard_map(
        functools.partial(on_device, nz, mesh.shape["expert"]),
        mesh=mesh, in_specs=in_specs, out_specs=P("dp", None), check_vma=False,
    )
```

```python
import functools

import jax
import jax.numpy as jnp
from jax import lax
from jax.experimental import pallas as pl
from jax.experimental.pallas import tpu as pltpu
from jax.sharding import PartitionSpec as P

NX = 4
Q = 2
MESH = pl.DeviceIdType.MESH
F32 = jnp.float32
BF16 = jnp.bfloat16


def moe_kernel(
    nz, ny, ids_hbm, levels_hbm, tok_hbm, w_gate, w_up, w_down, out,
    ids, levels, tok, wgu, wd, comp, comp_in, mix, mix_in, grid, part, part_in, near, far_in, merged,
    x_in, z_out, z_in, fin, half_out, half_in,
    in_sem, w_sem, c_s, c_r, zg_s, zg_r, xg_s, xg_r, xf_s, xf_r, pg_s, pg_r, ps_s, ps_r,
    xs_s, xs_r, zs_s, zs_r, y_s, y_r,
):
    dp = lax.axis_index("dp")
    y = lax.axis_index("expert")
    c = lax.rem(dp, 2)
    x = lax.rem(dp // 2, NX)
    z = dp // (2 * NX)
    oc = 1 - c
    half = tok.shape[1] // 2
    quarter = half // Q
    hz = nz // 2
    xl, xr, xo = lax.rem(x + NX - 1, NX), lax.rem(x + 1, NX), lax.rem(x + 2, NX)

    def dev(zz, xx, cc):
        return ((zz * NX + xx) * 2 + cc, y)

    partner, left, right = dev(z, x, oc), dev(z, xl, c), dev(z, xr, c)
    opposite = dev(z, xo, c)
    z_to = [dev(lax.rem(z + d, nz), x, c) for d in range(nz)]
    y_to = [(dp, lax.rem(y + d, ny)) for d in range(ny)]
    sent = []

    def desc(src, dst, s, r, to):
        return pltpu.make_async_remote_copy(
            src_ref=src, dst_ref=dst, send_sem=s, recv_sem=r, device_id=to, device_id_type=MESH
        )

    def send(src, dst, s, r, to):
        copy = desc(src, dst, s, r, to)
        copy.start()
        sent.append(copy)

    def flush(count):
        for copy in sent[:count]:
            copy.wait_send()
        del sent[:count]

    def arrived(dst, s, r, to):
        desc(dst, dst, s, r, to).wait_recv()

    small = [
        pltpu.make_async_copy(ids_hbm, ids, in_sem.at[0]),
        pltpu.make_async_copy(levels_hbm, levels, in_sem.at[1]),
        pltpu.make_async_copy(tok_hbm, tok, in_sem.at[2]),
    ]
    for load in small:
        load.start()

    barrier = pltpu.get_barrier_semaphore()
    peers = [partner, left, right, opposite] + z_to[1:] + y_to[1:]
    for peer in peers:
        pl.semaphore_signal(barrier, inc=1, device_id=peer, device_id_type=MESH)

    n_own, ff = w_gate.shape[0], w_gate.shape[2]
    loads = []
    for l in range(n_own):
        loads += [
            pltpu.make_async_copy(w_gate.at[l], wgu.at[l, :, pl.ds(0, ff)], w_sem.at[4 * l]),
            pltpu.make_async_copy(w_up.at[l], wgu.at[l, :, pl.ds(ff, ff)], w_sem.at[4 * l + 1]),
        ]
        for h in range(2):
            loads.append(
                pltpu.make_async_copy(
                    w_down.at[l, :, pl.ds(h * half, half)],
                    wd.at[h, pl.ds(l * ff, ff)],
                    w_sem.at[4 * l + 2 + h],
                )
            )
    for load in loads:
        load.start()
    for load in small:
        load.wait()

    n_rows = tok.shape[0]
    row = lax.broadcasted_iota(jnp.int32, (8, 128), 0)
    lane = lax.broadcasted_iota(jnp.int32, (8, 128), 1)
    expert_row = 2 * y + row // 4
    here_row = (row % 4) // 2 == c
    slot_row = row % 2
    expert_lane = 2 * (lane // 8) + (lane % 8) // 4
    here_lane = (lane % 4) // 2 == c
    slot_lane = lane % 2
    seen = jnp.zeros((8, 128), jnp.int32)
    tokens = tok[...].astype(F32)
    compact = jnp.zeros((8, 2 * half), F32)
    for t in range(n_rows):
        id0 = jnp.full((8, 128), ids[0, t], jnp.int32)
        id1 = jnp.full((8, 128), ids[1, t], jnp.int32)
        hit = (id0 == expert_row) | (id1 == expert_row)
        take = hit & (seen == slot_row) & here_row
        seen = seen + hit.astype(jnp.int32)
        factor = jnp.where(take, 1.0, 0.0).astype(F32)[:, :1]
        compact = compact + factor * tokens[t : t + 1, :]
    comp[0] = compact[:, :half].astype(BF16)
    comp[1] = compact[:, half:].astype(BF16)

    pl.semaphore_wait(barrier, len(peers))

    send(comp.at[oc], comp_in, c_s.at[0], c_r.at[0], partner)
    arrived(comp_in, c_s.at[0], c_r.at[0], partner)
    grid[c, x, z] = (comp[c].astype(F32) + comp_in[...].astype(F32)).astype(BF16)

    order = sorted(range(nz), key=lambda d: (min(d, nz - d), d))
    z_src = [lax.rem(z + nz - d, nz) for d in range(nz)]
    for d in reversed(order[1:]):
        send(grid.at[c, x, z], grid.at[c, x, z], zg_s.at[d], zg_r.at[d], z_to[d])

    seen = jnp.zeros((8, 128), jnp.int32)
    weights = jnp.zeros((8, 128), F32)
    for t in range(n_rows):
        hit0 = jnp.full((8, 128), ids[0, t], jnp.int32) == expert_lane
        hit1 = jnp.full((8, 128), ids[1, t], jnp.int32) == expert_lane
        lev0 = jnp.full((8, 128), levels[0, t], jnp.int32).astype(F32)
        lev1 = jnp.full((8, 128), levels[1, t], jnp.int32).astype(F32)
        hit = hit0 | hit1
        take = hit & (seen == slot_lane) & here_lane & (row == t)
        seen = seen + hit.astype(jnp.int32)
        weights = jnp.where(take, jnp.where(hit0, lev0, lev1) / (lev0 + lev1), weights)
    mix[...] = weights
    send(mix, mix_in, c_s.at[1], c_r.at[1], partner)

    def relay(i):
        d = order[i]
        side = i % 2
        src = grid.at[c, (xl, xr)[side], z_src[d]]
        to = (right, left)[side]
        arrived(src, xg_s.at[side, d], xg_r.at[side, d], to)
        send(src, src, xf_s.at[d], xf_r.at[d], to)

    lag = 3
    n_relay = min(nz, 5)
    for i, d in enumerate(order):
        block = grid.at[c, x, z_src[d]]
        if i:
            arrived(block, zg_s.at[d], zg_r.at[d], z_to[d])
        send(block, block, xg_s.at[0, d], xg_r.at[0, d], right)
        send(block, block, xg_s.at[1, d], xg_r.at[1, d], left)
        if i >= n_relay:
            send(block, block, xf_s.at[d], xf_r.at[d], opposite)
        if lag <= i < n_relay + lag:
            relay(i - lag)
    send(grid.at[c, x], grid.at[c, x], pg_s.at[0], pg_r.at[0], partner)
    for i in range(max(nz - lag, 0), n_relay):
        relay(i)

    def swap_in(k, xx):
        send(grid.at[c, xx], grid.at[c, xx], pg_s.at[k], pg_r.at[k], partner)

    for side, xx in ((0, xl), (1, xr)):
        for i, d in enumerate(order):
            if i % 2 != side or i >= n_relay:
                arrived(
                    grid.at[c, xx, z_src[d]], xg_s.at[side, d], xg_r.at[side, d], (right, left)[side]
                )
        swap_in(1 + side, xx)

    rows = nz * 8
    own_row = (lax.broadcasted_iota(jnp.int32, (rows, ff), 0) % 8) // 4

    def compute(k, xx):
        if k == 3:
            for d in order:
                far = grid.at[oc, xo, z_src[d]]
                arrived(far, pg_s.at[3 + d], pg_r.at[3 + d], partner)
        else:
            arrived(grid.at[oc, xx], pg_s.at[k], pg_r.at[k], partner)
        block0 = grid[0, xx].astype(F32).reshape(rows, half).astype(BF16)
        block1 = grid[1, xx].astype(F32).reshape(rows, half).astype(BF16)
        parts = []
        for l in range(n_own):
            both = jnp.dot(block0, wgu[l, :half, :], preferred_element_type=F32)
            both = both + jnp.dot(block1, wgu[l, half:, :], preferred_element_type=F32)
            gate, up = both[:, :ff], both[:, ff:]
            hidden = gate / (1.0 + jnp.exp(-gate)) * up
            parts.append(jnp.where(own_row == l, hidden, 0.0).astype(BF16))
        hidden = jnp.concatenate(parts, axis=1)
        for h in (oc, c):
            result = jnp.dot(hidden, wd[h], preferred_element_type=F32).reshape(nz, 8, half)
            for q in range(Q):
                part[k, h, q] = result[:, :, q * quarter : (q + 1) * quarter].astype(BF16)
                if h is oc:
                    send(part.at[k, oc, q], part_in.at[k, q], ps_s.at[k, q], ps_r.at[k, q], partner)

    def pair_sum(k, q):
        arrived(part_in.at[k, q], ps_s.at[k, q], ps_r.at[k, q], partner)
        return part[k, c, q].astype(F32) + part_in[k, q].astype(F32)

    for load in loads:
        load.wait()
    compute(0, x)
    for d in order:
        far = grid.at[c, xo, z_src[d]]
        arrived(far, xf_s.at[d], xf_r.at[d], right)
        send(far, far, pg_s.at[3 + d], pg_r.at[3 + d], partner)
    compute(1, xl)
    compute(2, xr)
    compute(3, xo)

    low, high = pl.ds(0, hz), pl.ds(hz, hz)
    gathered = len(sent)

    def near_send(q):
        send(near.at[0, q, low], x_in.at[1, q, low], xs_s.at[0, q], xs_r.at[0, q], left)
        send(near.at[1, q, high], x_in.at[0, q, high], xs_s.at[1, q], xs_r.at[1, q], right)

    for q in range(Q):
        near[0, q] = pair_sum(1, q).astype(BF16)
        near[1, q] = pair_sum(2, q).astype(BF16)
        if q == 0:
            near_send(q)
    for q in range(Q):
        near[2, q] = pair_sum(3, q).astype(BF16)
        send(near.at[2, q, low], far_in.at[0, q], xs_s.at[2, q], xs_r.at[2, q], right)
        send(near.at[2, q, high], far_in.at[1, q], xs_s.at[3, q], xs_r.at[3, q], left)
    for q in range(1, Q):
        near_send(q)
    flush(gathered)
    for q in range(Q):
        arrived(far_in.at[0, q], xs_s.at[2, q], xs_r.at[2, q], right)
        merged[0, q] = (near[1, q, :hz].astype(F32) + far_in[0, q].astype(F32)).astype(BF16)
        send(merged.at[0, q], x_in.at[0, q, low], xs_s.at[4, q], xs_r.at[4, q], right)
        arrived(far_in.at[1, q], xs_s.at[3, q], xs_r.at[3, q], left)
        merged[1, q] = (near[0, q, hz:].astype(F32) + far_in[1, q].astype(F32)).astype(BF16)
        send(merged.at[1, q], x_in.at[1, q, high], xs_s.at[5, q], xs_r.at[5, q], left)

    summed = len(sent)
    for q in range(Q):
        total = pair_sum(0, q)
        arrived(x_in.at[1, q, low], xs_s.at[0, q], xs_r.at[0, q], left)
        arrived(x_in.at[0, q, high], xs_s.at[1, q], xs_r.at[1, q], right)
        arrived(x_in.at[0, q, low], xs_s.at[4, q], xs_r.at[4, q], right)
        arrived(x_in.at[1, q, high], xs_s.at[5, q], xs_r.at[5, q], left)
        z_out[q] = (total + x_in[0, q].astype(F32) + x_in[1, q].astype(F32)).astype(BF16)
        for d in reversed(order[1:]):
            send(
                z_out.at[q, lax.rem(z + d, nz)], z_in.at[q, d], zs_s.at[q, d], zs_r.at[q, d], z_to[d]
            )

    flush(summed)
    shared = len(sent)
    y_order = sorted(range(1, ny), key=lambda d: -min(d, ny - d))
    for q in range(Q):
        final = z_out[q, z].astype(F32)
        for d in order[1:]:
            arrived(z_in.at[q, d], zs_s.at[q, d], zs_r.at[q, d], z_to[d])
            final = final + z_in[q, d].astype(F32)
        fin[q, y] = final.astype(BF16)
        for d in y_order:
            send(fin.at[q, y], fin.at[q, y], y_s.at[q, d], y_r.at[q, d], y_to[d])

    flush(shared)
    arrived(mix_in, c_s.at[1], c_r.at[1], partner)
    gates = jnp.concatenate([mix[...], mix_in[...]], axis=0)
    terms = []
    for _ in range(3):
        term = gates.astype(BF16).astype(F32)
        gates = gates - term
        terms.append(term)
    terms = jnp.concatenate(terms, axis=0)[:, : ny * 8].astype(BF16)
    mine = []
    spread = len(sent)
    for q in range(Q):
        for d in reversed(y_order):
            arrived(fin.at[q, lax.rem(y + ny - d, ny)], y_s.at[q, d], y_r.at[q, d], y_to[d])
        values = fin[q].astype(F32).reshape(ny * 8, quarter).astype(BF16)
        mixed = jnp.dot(terms, values, preferred_element_type=F32)
        mixed = mixed[32:] + mixed[16:32] + mixed[:16]
        half_out[q] = mixed[8:].astype(BF16)
        send(half_out.at[q], half_in.at[q], c_s.at[2 + q], c_r.at[2 + q], partner)
        mine.append(mixed[:8])
    flush(spread)
    for q in range(Q):
        arrived(half_in.at[q], c_s.at[2 + q], c_r.at[2 + q], partner)
        theirs = half_in[q].astype(F32)
        first, second = q * quarter, half + q * quarter
        out[:, first : first + quarter] = jnp.where(c == 0, mine[q], theirs).astype(BF16)
        out[:, second : second + quarter] = jnp.where(c == 0, theirs, mine[q]).astype(BF16)
    flush(len(sent))


def on_device(nz, ny, tokens, expert_ids, gate_levels, w_gate, w_up, w_down):
    width = tokens.shape[1]
    half = width // 2
    n_own, _, ff = w_gate.shape
    hz = nz // 2
    vmem, smem, dma = pltpu.VMEM, pltpu.SMEM, pltpu.SemaphoreType.DMA
    quarter = half // Q
    scratch = [
        smem((2, tokens.shape[0]), jnp.int32),
        smem((2, tokens.shape[0]), jnp.int32),
        vmem(tokens.shape, BF16),
        vmem((n_own, width, 2 * ff), BF16),
        vmem((2, n_own * ff, half), BF16),
        vmem((2, 8, half), BF16),
        vmem((8, half), BF16),
        vmem((8, 128), F32),
        vmem((8, 128), F32),
        vmem((2, NX, nz, 8, half), BF16),
        vmem((4, 2, Q, nz, 8, quarter), BF16),
        vmem((4, Q, nz, 8, quarter), BF16),
        vmem((3, Q, nz, 8, quarter), BF16),
        vmem((2, Q, hz, 8, quarter), BF16),
        vmem((2, Q, hz, 8, quarter), BF16),
        vmem((2, Q, nz, 8, quarter), BF16),
        vmem((Q, nz, 8, quarter), BF16),
        vmem((Q, nz, 8, quarter), BF16),
        vmem((Q, ny, 8, quarter), BF16),
        vmem((Q, 8, quarter), BF16),
        vmem((Q, 8, quarter), BF16),
        dma((3,)),
        dma((4 * n_own,)),
        dma((2 + Q,)), dma((2 + Q,)),
        dma((nz,)), dma((nz,)),
        dma((2, nz)), dma((2, nz)),
        dma((nz,)), dma((nz,)),
        dma((3 + nz,)), dma((3 + nz,)),
        dma((4, Q)), dma((4, Q)),
        dma((6, Q)), dma((6, Q)),
        dma((Q, nz)), dma((Q, nz)),
        dma((Q, ny)), dma((Q, ny)),
    ]
    return pl.pallas_call(
        functools.partial(moe_kernel, nz, ny),
        out_shape=jax.ShapeDtypeStruct(tokens.shape, BF16),
        in_specs=[pl.BlockSpec(memory_space=pl.ANY)] * 6,
        out_specs=pl.BlockSpec(memory_space=vmem),
        scratch_shapes=scratch,
        compiler_params=pltpu.CompilerParams(
            collective_id=0, has_side_effects=True, vmem_limit_bytes=67043328
        ),
    )(expert_ids.T, gate_levels.T, tokens, w_gate, w_up, w_down)


def solution(mesh):
    nz = mesh.shape["dp"] // (2 * NX)
    in_specs = (
        P("dp", None),
        P("dp", None),
        P("dp", None),
        P("expert", None, "dp"),
        P("expert", None, "dp"),
        P("expert", "dp", None),
    )
    return jax.shard_map(
        functools.partial(on_device, nz, mesh.shape["expert"]),
        mesh=mesh, in_specs=in_specs, out_specs=P("dp", None), check_vma=False,
    )
```
